32 devices in a mesh: lat: 4 (over y, x), lon: 8 (over z, core).
Axes of the slice: x: 2, y: 2, z: 4, core: 2. Of those that a mesh axis runs over, the one named last changes fastest.
Arguments:
- increment: float32 [4, 20, 128, 512], P(None, None, 'lon', 'lat'), may hold values from -6 to 6
- obs_dep: float32 [4, 20, 128, 512], P(None, None, 'lon', 'lat'), may hold values from -6 to 6
- obs_weight: float32 [4, 20, 128, 512], P(None, None, 'lon', 'lat'), may hold values from 0.1 to 10
- dep_lon: int32 [20, 128, 512], P(None, 'lon', 'lat'), may hold values from -5 to 5
- dep_lat: int32 [20, 128, 512], P(None, 'lon', 'lat'), may hold values from -5 to 5
- frac_lon: float32 [20, 128, 512], P(None, 'lon', 'lat'), may hold values from 0 to 1
- frac_lat: float32 [20, 128, 512], P(None, 'lon', 'lat'), may hold values from 0 to 1
- coupling: float32 [4, 19, 128, 512], P(None, None, 'lon', 'lat'), may hold values from 0.05 to 5
Outputs:
- tl_out: float32 [4, 20, 128, 512], P(None, None, 'lon', 'lat')
- gradient: float32 [4, 20, 128, 512], P(None, None, 'lon', 'lat')
The draws below stay inside these ranges and needn't reach their ends.
All inputs are finite; a program needn't handle non-finite values.
Results may differ from the reference program's by a relative error of at most 0.0003.
Values sent between devices are 32-bit elements; how exact they have to be, the bound alone decides.
A program may use at most 128 MiB of HBM per device.

```python
import math
import jax
import jax.numpy as jnp
from jax import lax

F = 4
LEV = 20
HALO = 6
NLON = 128
NLAT = 512


def touch_ends(array, own_key, least, top_value):
    extent = array.shape
    index_at = [jax.random.randint(jax.random.fold_in(own_key, axis), (), 0, extent[axis]) for axis in range(len(extent))]
    array = array.at[tuple(index_at)].set(least)
    longest = extent.index(max(extent))
    index_at[longest] = (index_at[longest] + 1) % extent[longest]
    return array.at[tuple(index_at)].set(top_value)


def block_levels(rng, dims, cuts, least, top_value):
    def one(dim, blocks):
        heights = jax.random.uniform(jax.random.fold_in(jax.random.fold_in(rng, 6), dim), (blocks,), jnp.float32, least / len(cuts), top_value / len(cuts))
        return jnp.repeat(jnp.exp(heights), dims[dim] // blocks).reshape((-1,) + (1,) * (len(dims) - dim - 1))

    loudness = one(*cuts[0])
    for cut in cuts[1:]:
        loudness = loudness * one(*cut)
    return loudness


def scatter_about(key, dims, width, limit, cuts=(), held_as=jnp.bfloat16):
    gain = block_levels(key, dims, cuts, -0.22, 0.18) if cuts else 1.0
    values = jax.random.normal(key, dims, jnp.float32) * width * gain
    return jnp.minimum(jnp.maximum(values, -limit), limit).astype(held_as)


def setup_inputs(seed: int = 0) -> dict:
    splits = jax.random.split(jax.random.key(seed), 9)
    increment = scatter_about(splits[0], (F, LEV, NLON, NLAT), 1.0, 6.0, ((2, 8), (3, 4)), jnp.float32)
    obs_dep = scatter_about(splits[1], (F, LEV, NLON, NLAT), 1.0, 6.0, ((2, 8), (3, 4)), jnp.float32)
    obs_weight = jnp.clip(jnp.exp(math.log(10.0) - 4.6051702 * jax.random.uniform(splits[2], (F, LEV, NLON, NLAT), jnp.float32) ** block_levels(splits[2], (F, LEV, NLON, NLAT), ((2, 8), (3, 4)), -0.2, 0.2)), 0.1, 10.0)
    dep_lon = touch_ends(jax.random.randint(splits[3], (LEV, NLON, NLAT), 1 - HALO, HALO), jax.random.fold_in(splits[3], 1), 1 - HALO, HALO - 1).astype(jnp.int32)
    dep_lat = touch_ends(jax.random.randint(splits[4], (LEV, NLON, NLAT), 1 - HALO, HALO), jax.random.fold_in(splits[4], 1), 1 - HALO, HALO - 1).astype(jnp.int32)
    frac_lon = jnp.clip(1.0 * jax.random.uniform(splits[5], (LEV, NLON, NLAT), jnp.float32) ** block_levels(splits[5], (LEV, NLON, NLAT), ((1, 8), (2, 4)), -0.2, 0.2), 0.0, 1.0)
    frac_lat = jnp.clip(1.0 * jax.random.uniform(splits[6], (LEV, NLON, NLAT), jnp.float32) ** block_levels(splits[6], (LEV, NLON, NLAT), ((1, 8), (2, 4)), -0.2, 0.2), 0.0, 1.0)
    coupling = jnp.clip(jnp.exp(math.log(5.0) - 4.6051702 * jax.random.uniform(splits[7], (F, LEV - 1, NLON, NLAT), jnp.float32) ** block_levels(splits[7], (F, LEV - 1, NLON, NLAT), ((2, 8), (3, 4)), -0.2, 0.2)), 0.05, 5.0)
    return {"increment": increment, "obs_dep": obs_dep, "obs_weight": obs_weight, "dep_lon": dep_lon, "dep_lat": dep_lat, "frac_lon": frac_lon, "frac_lat": frac_lat, "coupling": coupling}


def column_solve(rhs, coup):
    levels = rhs.shape[1]
    nothing = jnp.zeros_like(rhs[:, 0])
    ratios = []
    primes = []
    for level in range(levels):
        below = coup[:, level - 1] if level > 0 else nothing
        above = coup[:, level] if level < levels - 1 else nothing
        diagonal = 1.0 + below + above
        if level == 0:
            denom = diagonal
            prime = rhs[:, 0] / denom
        else:
            denom = diagonal - below * ratios[-1]
            prime = (rhs[:, level] + below * primes[-1]) / denom
        ratios.append(above / denom)
        primes.append(prime)
    result = [primes[-1]]
    for level in range(levels - 2, -1, -1):
        result.append(primes[level] + ratios[level] * result[-1])
    ordered = result[::-1]
    return jnp.stack(ordered, axis=1)


def level_pairs(olon, olat, flon, flat):
    lon_index = lax.broadcasted_iota(jnp.int32, (NLON, NLAT), 0)
    lat_index = lax.broadcasted_iota(jnp.int32, (NLON, NLAT), 1)
    pairs = []
    for lon_step in (0, 1):
        weight_lon = 1.0 - flon if lon_step == 0 else flon
        for lat_step in (0, 1):
            weight_lat = 1.0 - flat if lat_step == 0 else flat
            lon_src = jnp.mod(lon_index - olon - lon_step, NLON)
            lat_src = lat_index - olat - lat_step
            inside = (lat_src >= 0) & (lat_src < NLAT)
            target = (lon_src * NLAT + jnp.clip(lat_src, 0, NLAT - 1)).astype(jnp.int32)
            weight = jnp.where(inside, weight_lon * weight_lat, jnp.zeros_like(flon))
            pairs.append((target.reshape(-1), weight.reshape(-1)))
    return pairs


def forward_level(args):
    field, olon, olat, flon, flat = args
    fields = field.shape[0]
    flat_src = field.reshape(fields, -1)
    terms = [weight[None] * flat_src[:, target] for target, weight in level_pairs(olon, olat, flon, flat)]
    summed = terms[0] + terms[1] + terms[2] + terms[3]
    return summed.reshape(fields, NLON, NLAT)


def backward_level(args):
    field, olon, olat, flon, flat = args
    fields = field.shape[0]
    values = field.reshape(fields, -1)
    spread = jnp.zeros_like(values)
    for target, weight in level_pairs(olon, olat, flon, flat):
        spread = spread.at[:, target].add(weight[None] * values)
    return spread.reshape(fields, NLON, NLAT)


def reference(increment, obs_dep, obs_weight, dep_lon, dep_lat, frac_lon, frac_lat, coupling):
    by_level = jnp.moveaxis(increment, 1, 0)
    advected = jnp.moveaxis(lax.map(forward_level, (by_level, dep_lon, dep_lat, frac_lon, frac_lat)), 0, 1)
    tl_out = column_solve(advected, coupling)
    forcing = obs_weight * (tl_out - obs_dep)
    smoothed = column_solve(forcing, coupling)
    adjoint = jnp.moveaxis(lax.map(backward_level, (jnp.moveaxis(smoothed, 1, 0), dep_lon, dep_lat, frac_lon, frac_lat)), 0, 1)
    gradient = increment + adjoint
    return (tl_out, gradient)
```

```python
import functools

import jax
import jax.numpy as jnp
from jax import lax
from jax.experimental import pallas as pl
from jax.experimental.pallas import tpu as pltpu
from jax.sharding import PartitionSpec as P

HALO = 6
SHIFTS = tuple(range(1 - HALO, HALO + 1))
LANES = 128
SLOT = 16
PER = LANES // SLOT
MESH = pl.DeviceIdType.MESH
ANY = pl.BlockSpec(memory_space=pl.ANY)
VMEM = pl.BlockSpec(memory_space=pltpu.VMEM)
LIMIT = 56 * 1024 * 1024


def lane_index(shape):
    return lax.broadcasted_iota(jnp.int32, shape, len(shape) - 1)


def roll(x, shift):
    return pltpu.roll(x, shift, x.ndim - 1)


def neighbours(sizes):
    lat, lon = lax.axis_index("lat"), lax.axis_index("lon")

    def at(dy, dx):
        return {
            "lat": lax.rem(lat + dy + sizes[0], sizes[0]),
            "lon": lax.rem(lon + dx + sizes[1], sizes[1]),
        }

    return at


def greet(devices):
    barrier = pltpu.get_barrier_semaphore()
    for device in devices:
        pl.semaphore_signal(barrier, inc=1, device_id=device, device_id_type=MESH)
    pl.semaphore_wait(barrier, len(devices))


def remote(src, dst, send, recv, number, device):
    return pltpu.make_async_remote_copy(
        src_ref=src,
        dst_ref=dst,
        send_sem=send.at[number],
        recv_sem=recv.at[number],
        device_id=device,
        device_id_type=MESH,
    )


def pack_edges(src, dst):
    @pl.loop(0, dst.shape[0])
    def _(group):
        total = None
        for e in range(PER):
            x = src[group * PER + e]
            lane = lane_index(x.shape)
            x = jnp.where((lane < HALO) | (lane >= LANES - HALO), x, 0.0)
            x = roll(x, (HALO + SLOT * e) % LANES)
            total = x if total is None else total + x
        dst[group] = total


def increment_exchange(sizes, inc, from_left, from_right, edges, local, packed, send, recv, here):
    at = neighbours(sizes)
    own = pltpu.make_async_copy(inc, local, here)
    own.start()
    greet([at(dy, dx) for dy in (-1, 0, 1) for dx in (-1, 0, 1) if (dy, dx) != (0, 0)])
    copies = [
        remote(inc.at[:, 0:8], from_right, send, recv, 0, at(0, -1)),
        remote(inc.at[:, 8:16], from_left, send, recv, 1, at(0, 1)),
    ]
    for copy in copies:
        copy.start()
    own.wait()
    pack_edges(local, packed)
    number = 2
    for dy in (-1, 1):
        side = 0 if dy == 1 else 1
        for dx in (0, -1, 1):
            rows, into = {0: ((0, 16), 8), -1: ((0, 8), 24), 1: ((8, 16), 0)}[dx]
            copy = remote(
                packed.at[:, rows[0] : rows[1]],
                edges.at[side, :, into : into + rows[1] - rows[0]],
                send,
                recv,
                number,
                at(dy, dx),
            )
            copy.start()
            copies.append(copy)
            number += 1
    for copy in copies:
        copy.wait()


def sector_exchange(sizes, z, from_left, from_right, send, recv):
    at = neighbours(sizes)
    greet([at(0, -1), at(0, 1)])
    copies = [
        remote(z.at[:, 0:8], from_right, send, recv, 0, at(0, -1)),
        remote(z.at[:, 8:16], from_left, send, recv, 1, at(0, 1)),
    ]
    for copy in copies:
        copy.start()
    for copy in copies:
        copy.wait()


def band_exchange(sizes, packed, edges, send, recv):
    at = neighbours(sizes)
    greet([at(-1, 0), at(1, 0)])
    copies = [
        remote(packed, edges.at[1], send, recv, 0, at(-1, 0)),
        remote(packed, edges.at[0], send, recv, 1, at(1, 0)),
    ]
    for copy in copies:
        copy.start()
    for copy in copies:
        copy.wait()


def store_weights(dst, offset, frac):
    rest = 1.0 - frac
    before = None
    for pos, total in enumerate(SHIFTS):
        here = offset == total
        second = 0.0 if before is None else jnp.where(before, frac, 0.0)
        dst[pos] = jnp.where(here, rest, second)
        before = here


def forward_kernel(
    dims, bands, inc, from_left, from_right, edges, dep, weight, olon, olat, flon, flat, coup,
    tl, z, shifted, lonw, latw, prime, ratio, inverse,
):
    fields, levels = dims
    band = lax.axis_index("lat")
    has_lower = band > 0
    has_upper = band < bands - 1

    @pl.loop(0, levels)
    def _(k):
        store_weights(lonw, olon[k], flon[k])
        store_weights(latw, olat[k], flat[k])

        @pl.loop(0, fields)
        def _(f):
            at = f * levels + k
            main = jnp.concatenate([from_left[at], inc[at], from_right[at]], axis=0)
            group, slot = at // PER, at % PER
            shift = lax.rem(2 * LANES - HALO - SLOT * slot, LANES)
            lane = lane_index(main.shape)
            lower = jnp.where(has_lower, roll(edges[0, group], shift), 0.0)
            upper = jnp.where(has_upper, roll(edges[1, group], shift), 0.0)
            edge = jnp.where(lane < LANES // 2, upper, lower)
            for pos, total in enumerate(SHIFTS):
                t = -total
                if t == 0:
                    shifted[pos] = main
                    continue
                inside = (lane >= LANES + t) if t < 0 else (lane < t)
                shifted[pos] = roll(jnp.where(inside, edge, main), (-t) % LANES)
            c = f * (levels - 1) + k
            first, last = k == 0, k == levels - 1
            for half in range(2):
                rows = pl.ds(8 * half, 8)
                lat = [latw[pos, rows] for pos in range(len(SHIFTS))]
                adv = None
                for lon_pos, lon_total in enumerate(SHIFTS):
                    inner = None
                    start = 8 + 8 * half - lon_total
                    for pos in range(len(SHIFTS)):
                        term = lat[pos] * shifted[pos, pl.ds(start, 8)]
                        inner = term if inner is None else inner + term
                    term = lonw[lon_pos, rows] * inner
                    adv = term if adv is None else adv + term
                below = jnp.where(first, 0.0, coup[jnp.where(first, c, c - 1), rows])
                above = jnp.where(last, 0.0, coup[jnp.where(last, c - 1, c), rows])
                prev = jnp.where(first, at, at - 1)
                ratio_prev = jnp.where(first, 0.0, ratio[prev, rows])
                prime_prev = jnp.where(first, 0.0, prime[prev, rows])
                inv = 1.0 / (1.0 + below + above - below * ratio_prev)
                inverse[at, rows] = inv
                ratio[at, rows] = above * inv
                prime[at, rows] = (adv + below * prime_prev) * inv

    @pl.loop(0, fields)
    def _(f):
        base = f * levels
        x = prime[base + levels - 1]
        tl[base + levels - 1] = x
        for k in range(levels - 2, -1, -1):
            x = prime[base + k] + ratio[base + k] * x
            tl[base + k] = x
        kept = []
        for k in range(levels):
            at = base + k
            forcing = weight[at] * (tl[at] - dep[at])
            if k > 0:
                forcing = forcing + coup[f * (levels - 1) + k - 1] * kept[-1]
            kept.append(forcing * inverse[at])
        x = kept[-1]
        z[base + levels - 1] = x
        for k in range(levels - 2, -1, -1):
            x = kept[k] + ratio[base + k] * x
            z[base + k] = x


def adjoint_kernel(
    dims, inc, z, z_left, z_right, olon, olat, flon, flat, g_left, g_right,
    grad, packed, lonw, latw, wide, spill,
):
    fields, levels = dims
    lane = lane_index((8, LANES))

    def widened(own, number, k):
        left, right = g_left[number, k], g_right[number, k]
        return jnp.concatenate([left, own[k].astype(jnp.float32), right], axis=0)

    @pl.loop(0, levels)
    def _(k):
        store_weights(lonw, widened(olon, 0, k), widened(flon, 2, k))
        store_weights(latw, widened(olat, 1, k), widened(flat, 3, k))
        for f in range(fields):
            at = f * levels + k
            wide[f, 0:8] = z_left[at]
            wide[f, 8:24] = z[at]
            wide[f, 24:32] = z_right[at]
        for half in range(2):
            rows = pl.ds(8 * half, 8)
            for pair in range(0, fields, 2):
                both = range(pair, min(pair + 2, fields))
                sums = {}
                for lon_pos, lon_total in enumerate(SHIFTS):
                    near = pl.ds(8 + 8 * half + lon_total, 8)
                    scale = lonw[lon_pos, near]
                    scaled = {f: scale * wide[f, near] for f in both}
                    for pos in range(len(SHIFTS)):
                        w = latw[pos, near]
                        for f in both:
                            term = w * scaled[f]
                            sums[f, pos] = term if lon_pos == 0 else sums[f, pos] + term
                for f in both:
                    at = f * levels + k
                    total, outside = inc[at, rows], jnp.zeros((8, LANES), jnp.float32)
                    for pos, n in enumerate(SHIFTS):
                        if n == 0:
                            total = total + sums[f, pos]
                            continue
                        moved = roll(sums[f, pos], (-n) % LANES)
                        wraps = (lane >= LANES - n) if n > 0 else (lane < -n)
                        total = total + jnp.where(wraps, 0.0, moved)
                        outside = outside + jnp.where(wraps, moved, 0.0)
                    grad[at, rows] = total
                    spill[at, rows] = outside

    pack_edges(spill, packed)


def finish_kernel(bands, partial, edges, grad):
    band = lax.axis_index("lat")
    has_lower = band > 0
    has_upper = band < bands - 1
    lane = lane_index(partial.shape[1:])

    @pl.loop(0, edges.shape[1])
    def _(group):
        both = edges[0, group], edges[1, group]
        lower = jnp.where(has_lower, both[0], 0.0)
        upper = jnp.where(has_upper, both[1], 0.0)
        for e in range(PER):
            shift = (-HALO - SLOT * e) % LANES
            low = jnp.where(lane < HALO, roll(lower, shift), 0.0)
            high = jnp.where(lane >= LANES - HALO, roll(upper, shift), 0.0)
            at = group * PER + e
            grad[at] = partial[at] + (low + high)


def shards(sizes, increment, obs_dep, obs_weight, dep_lon, dep_lat, frac_lon, frac_lat, coupling):
    fields, levels, rows, cols = increment.shape
    count = fields * levels
    groups = count // PER
    dims = (fields, levels)
    f32 = jnp.float32

    def shape(*s):
        return jax.ShapeDtypeStruct(s, f32)

    def flat3(x):
        return x.reshape(-1, rows, cols)

    inc, dep, weight, coup = flat3(increment), flat3(obs_dep), flat3(obs_weight), flat3(coupling)
    tile = shape(count, 8, cols)
    whole = shape(count, rows, cols)

    from_left, from_right, edges = pl.pallas_call(
        functools.partial(increment_exchange, sizes),
        out_shape=(tile, tile, shape(2, groups, 32, cols)),
        in_specs=[ANY],
        out_specs=(ANY,) * 3,
        scratch_shapes=[
            pltpu.VMEM((count, rows, cols), f32),
            pltpu.VMEM((groups, rows, cols), f32),
            pltpu.SemaphoreType.DMA((8,)),
            pltpu.SemaphoreType.DMA((8,)),
            pltpu.SemaphoreType.DMA,
        ],
        compiler_params=pltpu.CompilerParams(collective_id=0, has_side_effects=True),
    )(inc)

    geometry = jnp.stack([dep_lon.astype(f32), dep_lat.astype(f32), frac_lon, frac_lat])
    n = sizes[1]
    g_left = lax.ppermute(geometry[:, :, 8:16], "lon", [(i, (i + 1) % n) for i in range(n)])
    g_right = lax.ppermute(geometry[:, :, 0:8], "lon", [((i + 1) % n, i) for i in range(n)])

    tl, z = pl.pallas_call(
        functools.partial(forward_kernel, dims, sizes[0]),
        out_shape=(whole, whole),
        in_specs=[VMEM] * 11,
        out_specs=(VMEM,) * 2,
        scratch_shapes=[
            pltpu.VMEM((12, 32, cols), f32),
            pltpu.VMEM((12, rows, cols), f32),
            pltpu.VMEM((12, rows, cols), f32),
            pltpu.VMEM((count, rows, cols), f32),
            pltpu.VMEM((count, rows, cols), f32),
            pltpu.VMEM((count, rows, cols), f32),
        ],
        compiler_params=pltpu.CompilerParams(vmem_limit_bytes=LIMIT),
        cost_estimate=pl.CostEstimate(flops=60_000_000, bytes_accessed=8_000_000, transcendentals=0),
    )(inc, from_left, from_right, edges, dep, weight, dep_lon, dep_lat, frac_lon, frac_lat, coup)

    z_left, z_right = pl.pallas_call(
        functools.partial(sector_exchange, sizes),
        out_shape=(tile, tile),
        in_specs=[ANY],
        out_specs=(ANY,) * 2,
        scratch_shapes=[pltpu.SemaphoreType.DMA((2,)), pltpu.SemaphoreType.DMA((2,))],
        compiler_params=pltpu.CompilerParams(collective_id=1, has_side_effects=True),
    )(z)

    partial, packed = pl.pallas_call(
        functools.partial(adjoint_kernel, dims),
        out_shape=(whole, shape(groups, rows, cols)),
        in_specs=[VMEM] * 10,
        out_specs=(VMEM,) * 2,
        scratch_shapes=[
            pltpu.VMEM((12, 32, cols), f32),
            pltpu.VMEM((12, 32, cols), f32),
            pltpu.VMEM((fields, 32, cols), f32),
            pltpu.VMEM((count, rows, cols), f32),
        ],
        compiler_params=pltpu.CompilerParams(vmem_limit_bytes=LIMIT),
    )(inc, z, z_left, z_right, dep_lon, dep_lat, frac_lon, frac_lat, g_left, g_right)

    back = pl.pallas_call(
        functools.partial(band_exchange, sizes),
        out_shape=shape(2, groups, rows, cols),
        in_specs=[ANY],
        out_specs=ANY,
        scratch_shapes=[pltpu.SemaphoreType.DMA((2,)), pltpu.SemaphoreType.DMA((2,))],
        compiler_params=pltpu.CompilerParams(collective_id=2, has_side_effects=True),
    )(packed)

    grad = pl.pallas_call(
        functools.partial(finish_kernel, sizes[0]),
        out_shape=whole,
        in_specs=[VMEM] * 2,
        out_specs=VMEM,
        compiler_params=pltpu.CompilerParams(vmem_limit_bytes=LIMIT),
    )(partial, back)
    return tl.reshape(increment.shape), grad.reshape(increment.shape)


def solution(mesh):
    sizes = (mesh.shape["lat"], mesh.shape["lon"])
    wide = P(None, None, "lon", "lat")
    level = P(None, "lon", "lat")
    return jax.shard_map(
        functools.partial(shards, sizes),
        mesh=mesh,
        in_specs=(wide, wide, wide, level, level, level, level, wide),
        out_specs=(wide, wide),
        check_vma=False,
    )
```

```python
import functools

import jax
import jax.numpy as jnp
from jax import lax
from jax.experimental import pallas as pl
from jax.experimental.pallas import tpu as pltpu
from jax.sharding import PartitionSpec as P

HALO = 6
SHIFTS = tuple(range(1 - HALO, HALO + 1))
LANES = 128
SLOT = 16
PER = LANES // SLOT
QUAD = 4
PAIR = 2
MESH = pl.DeviceIdType.MESH
ANY = pl.BlockSpec(memory_space=pl.ANY)
LIMIT = 56 * 1024 * 1024


def lane_index(shape):
    return lax.broadcasted_iota(jnp.int32, shape, len(shape) - 1)


def roll(x, shift):
    return pltpu.roll(x, shift, x.ndim - 1)


def neighbours(sizes):
    lat, lon = lax.axis_index("lat"), lax.axis_index("lon")

    def at(dy, dx):
        return {
            "lat": lax.rem(lat + dy + sizes[0], sizes[0]),
            "lon": lax.rem(lon + dx + sizes[1], sizes[1]),
        }

    return at


def greet(devices):
    barrier = pltpu.get_barrier_semaphore()
    for device in devices:
        pl.semaphore_signal(barrier, inc=1, device_id=device, device_id_type=MESH)
    pl.semaphore_wait(barrier, len(devices))


def remote(src, dst, send, recv, number, device):
    return pltpu.make_async_remote_copy(
        src_ref=src,
        dst_ref=dst,
        send_sem=send.at[number],
        recv_sem=recv.at[number],
        device_id=device,
        device_id_type=MESH,
    )


def pack_edges(src, base, dst):
    @pl.loop(0, dst.shape[0])
    def _(group):
        total = None
        for e in range(PER):
            x = src[base + group * PER + e]
            lane = lane_index(x.shape)
            x = jnp.where((lane < HALO) | (lane >= LANES - HALO), x, 0.0)
            x = roll(x, (HALO + SLOT * e) % LANES)
            total = x if total is None else total + x
        dst[group] = total


def pack_rows(src, base, low, high):
    @pl.loop(0, low.shape[0])
    def _(block):
        for i in range(QUAD):
            at = base + block * QUAD + i
            to = pl.ds(HALO * i, HALO)
            low[block, to] = src[at, 0:HALO].astype(jnp.float32)
            high[block, to] = src[at, 16 - HALO : 16].astype(jnp.float32)


def unpack_rows(src, base, left, right, dst):
    @pl.loop(0, left.shape[0])
    def _(block):
        for i in range(QUAD):
            at = block * QUAD + i
            of = pl.ds(HALO * i, HALO)
            dst[at, 8 - HALO : 8] = left[block, of]
            dst[at, 8:24] = src[base + at]
            dst[at, 24 : 24 + HALO] = right[block, of]


def store_weights(dst, rows, offset, frac):
    rest = 1.0 - frac
    before = None
    for pos, total in enumerate(SHIFTS):
        here = offset == total
        second = 0.0 if before is None else jnp.where(before, frac, 0.0)
        dst[pos, rows] = jnp.where(here, rest, second)
        before = here


def factor(dims, coup, ratio, inverse):
    fields, levels = dims
    previous = [None] * fields
    for k in range(levels):
        for f in range(fields):
            at, c = f * levels + k, f * (levels - 1) + k
            denom = 1.0
            if k > 0:
                below = coup[c - 1]
                denom = denom + below
            if k < levels - 1:
                above = coup[c]
                denom = denom + above
            if k > 0:
                denom = denom - below * previous[f]
            inv = 1.0 / denom
            inverse[at] = inv
            if k < levels - 1:
                previous[f] = above * inv
                ratio[at] = previous[f]


def advect(dims, first_field, band, bands, wide, edges, lonw, latw, coup, inverse, shifted, prime):
    fields, levels = dims
    has_lower = band > 0
    has_upper = band < bands - 1

    @pl.loop(0, PAIR)
    def _(member):
        @pl.loop(0, levels)
        def _(k):
            local = member * levels + k
            f = first_field + member
            at = f * levels + k
            main = wide[local]
            group, slot = local // PER, local % PER
            shift = lax.rem(2 * LANES - HALO - SLOT * slot, LANES)
            lane = lane_index(main.shape)
            lower = jnp.where(has_lower, roll(edges[0, group], shift), 0.0)
            upper = jnp.where(has_upper, roll(edges[1, group], shift), 0.0)
            edge = jnp.where(lane < LANES // 2, upper, lower)
            for pos, total in enumerate(SHIFTS):
                t = -total
                if t == 0:
                    shifted[pos] = main
                    continue
                inside = (lane >= LANES + t) if t < 0 else (lane < t)
                shifted[pos] = roll(jnp.where(inside, edge, main), (-t) % LANES)
            c = f * (levels - 1) + k
            first = k == 0
            for half in range(2):
                rows = pl.ds(8 * half, 8)
                inner_rows = pl.ds(8 + 8 * half, 8)
                lat = [latw[k, pos, inner_rows] for pos in range(len(SHIFTS))]
                adv = None
                for lon_pos, lon_total in enumerate(SHIFTS):
                    inner = None
                    start = 8 + 8 * half - lon_total
                    for pos in range(len(SHIFTS)):
                        term = lat[pos] * shifted[pos, pl.ds(start, 8)]
                        inner = term if inner is None else inner + term
                    term = lonw[k, lon_pos, inner_rows] * inner
                    adv = term if adv is None else adv + term
                below = jnp.where(first, 0.0, coup[jnp.where(first, c, c - 1), rows])
                before = jnp.where(first, 0.0, prime[jnp.where(first, at, at - 1), rows])
                prime[at, rows] = (adv + below * before) * inverse[at, rows]


def solve(dims, first_field, prime, ratio, inverse, coup, dep, weight, tl, z):
    fields, levels = dims
    members = range(first_field, first_field + PAIR)
    x = {}
    for k in range(levels - 1, -1, -1):
        for f in members:
            at = f * levels + k
            x[f] = prime[at] if k == levels - 1 else prime[at] + ratio[at] * x[f]
            tl[at] = x[f]
    for k in range(levels):
        for f in members:
            at = f * levels + k
            forcing = weight[at] * (tl[at] - dep[at])
            if k > 0:
                forcing = forcing + coup[f * (levels - 1) + k - 1] * x[f]
            x[f] = forcing * inverse[at]
            prime[at] = x[f]
    for k in range(levels - 1, -1, -1):
        for f in members:
            at = f * levels + k
            x[f] = prime[at] if k == levels - 1 else prime[at] + ratio[at] * x[f]
            z[at] = x[f]


def collect(dims, first_field, wide, lonw, latw, inc, grad, spill):
    fields, levels = dims
    lane = lane_index((8, LANES))

    @pl.loop(0, levels)
    def _(k):
        for half in range(2):
            rows = pl.ds(8 * half, 8)
            sums = {}
            for lon_pos, lon_total in enumerate(SHIFTS):
                near = pl.ds(8 + 8 * half + lon_total, 8)
                scale = lonw[k, lon_pos, near]
                scaled = [scale * wide[f * levels + k, near] for f in range(PAIR)]
                for pos in range(len(SHIFTS)):
                    w = latw[k, pos, near]
                    for f in range(PAIR):
                        term = w * scaled[f]
                        sums[f, pos] = term if lon_pos == 0 else sums[f, pos] + term
            for f in range(PAIR):
                at = (first_field + f) * levels + k
                total, outside = inc[at, rows], jnp.zeros((8, LANES), jnp.float32)
                for pos, n in enumerate(SHIFTS):
                    if n == 0:
                        total = total + sums[f, pos]
                        continue
                    moved = roll(sums[f, pos], (-n) % LANES)
                    wraps = (lane >= LANES - n) if n > 0 else (lane < -n)
                    total = total + jnp.where(wraps, 0.0, moved)
                    outside = outside + jnp.where(wraps, moved, 0.0)
                grad[at, rows] = total
                spill[f * levels + k, rows] = outside


def finish(base, band, bands, edges, grad):
    has_lower = band > 0
    has_upper = band < bands - 1

    @pl.loop(0, edges.shape[1])
    def _(group):
        lower = jnp.where(has_lower, edges[0, group], 0.0)
        upper = jnp.where(has_upper, edges[1, group], 0.0)
        lane = lane_index(lower.shape)
        for e in range(PER):
            shift = (-HALO - SLOT * e) % LANES
            low = jnp.where(lane < HALO, roll(lower, shift), 0.0)
            high = jnp.where(lane >= LANES - HALO, roll(upper, shift), 0.0)
            at = base + group * PER + e
            grad[at] = grad[at] + (low + high)


def kernel(
    dims, sizes,
    inc_h, dep_h, weight_h, olon_h, olat_h, flon_h, flat_h, coup_h,
    tl_h, grad_h,
    inc, dep, weight, olon, olat, flon, flat, coup, tl, grad,
    low, high, from_left, from_right, edge_out, edge_in,
    g_low, g_high, g_left, g_right, z_low, z_high, z_left, z_right,
    back_out, back_in, spill, wide, shifted, lonw, latw, prime, ratio, inverse, z,
    load_sem, store_sem, send, recv,
):
    fields, levels = dims
    pairs = fields // PAIR
    per_pair = PAIR * levels
    at = neighbours(sizes)
    band, bands = lax.axis_index("lat"), sizes[0]
    numbers = iter(range(send.shape[0]))

    loads = [
        pltpu.make_async_copy(src, dst, load_sem.at[i])
        for i, (src, dst) in enumerate(
            [(inc_h, inc), (olon_h, olon), (olat_h, olat), (flon_h, flon), (flat_h, flat),
             (coup_h, coup), (dep_h, dep), (weight_h, weight)]
        )
    ]
    for load in loads:
        load.start()

    def launch(src, dst, device):
        copy = remote(src, dst, send, recv, next(numbers), device)
        copy.start()
        return copy

    greet([at(dy, dx) for dy in (-1, 0, 1) for dx in (-1, 0, 1) if (dy, dx) != (0, 0)])
    loads[0].wait()
    inward = []
    for pair in range(pairs):
        pack_rows(inc, pair * per_pair, low.at[pair], high.at[pair])
        copies = [
            launch(low.at[pair], from_right.at[pair], at(0, -1)),
            launch(high.at[pair], from_left.at[pair], at(0, 1)),
        ]
        packed = edge_out.at[pair]
        pack_edges(inc, pair * per_pair, packed)
        for dy in (-1, 1):
            side = edge_in.at[pair, 0 if dy == 1 else 1]
            copies.append(launch(packed, side.at[:, 8:24], at(dy, 0)))
            copies.append(launch(packed.at[:, 0:8], side.at[:, 24:32], at(dy, -1)))
            copies.append(launch(packed.at[:, 8:16], side.at[:, 0:8], at(dy, 1)))
        inward.append(copies)
    for load in loads[1:6]:
        load.wait()
    geometry = (olon, olat, flon, flat)
    blocks = levels // QUAD
    for i, own in enumerate(geometry):
        part = pl.ds(i * blocks, blocks)
        pack_rows(own, 0, g_low.at[part], g_high.at[part])
    around = [
        launch(g_low, g_right, at(0, -1)),
        launch(g_high, g_left, at(0, 1)),
    ]

    @pl.loop(0, levels)
    def _(k):
        store_weights(lonw.at[k], pl.ds(8, 16), olon[k], flon[k])
        store_weights(latw.at[k], pl.ds(8, 16), olat[k], flat[k])

    factor(dims, coup, ratio, inverse)
    for load in loads[6:]:
        load.wait()

    stores, across = [], []
    for pair in range(pairs):
        base = pair * per_pair
        for copy in inward[pair]:
            copy.wait()
        unpack_rows(inc, base, from_left.at[pair], from_right.at[pair], wide)
        advect(dims, pair * PAIR, band, bands, wide, edge_in.at[pair], lonw, latw, coup, inverse, shifted, prime)
        solve(dims, pair * PAIR, prime, ratio, inverse, coup, dep, weight, tl, z)
        pack_rows(z, base, z_low.at[pair], z_high.at[pair])
        across.append([
            launch(z_low.at[pair], z_right.at[pair], at(0, -1)),
            launch(z_high.at[pair], z_left.at[pair], at(0, 1)),
        ])
        part = pl.ds(base, per_pair)
        store = pltpu.make_async_copy(tl.at[part], tl_h.at[part], store_sem.at[pair])
        store.start()
        stores.append(store)

    for copy in around:
        copy.wait()

    @pl.loop(0, blocks)
    def _(block):
        for i in range(QUAD):
            k = block * QUAD + i
            of = pl.ds(HALO * i, HALO)
            for side, rows in ((g_left, pl.ds(8 - HALO, HALO)), (g_right, pl.ds(24, HALO))):
                parts = [side[number * blocks + block, of] for number in range(4)]
                store_weights(lonw.at[k], rows, parts[0], parts[2])
                store_weights(latw.at[k], rows, parts[1], parts[3])

    returned = []
    for pair in range(pairs):
        base = pair * per_pair
        for copy in across[pair]:
            copy.wait()
        unpack_rows(z, base, z_left.at[pair], z_right.at[pair], wide)
        collect(dims, pair * PAIR, wide, lonw, latw, inc, grad, spill)
        pack_edges(spill, 0, back_out.at[pair])
        returned.append([
            launch(back_out.at[pair], back_in.at[pair, 1], at(-1, 0)),
            launch(back_out.at[pair], back_in.at[pair, 0], at(1, 0)),
        ])
    for pair in range(pairs):
        base = pair * per_pair
        for copy in returned[pair]:
            copy.wait()
        finish(base, band, bands, back_in.at[pair], grad)
        part = pl.ds(base, per_pair)
        store = pltpu.make_async_copy(grad.at[part], grad_h.at[part], store_sem.at[pairs + pair])
        store.start()
        stores.append(store)
    for store in stores:
        store.wait()


def shards(sizes, increment, obs_dep, obs_weight, dep_lon, dep_lat, frac_lon, frac_lat, coupling):
    fields, levels, rows, cols = increment.shape
    count = fields * levels
    pairs = fields // PAIR
    groups = PAIR * levels // PER
    quads = PAIR * levels // QUAD
    dims = (fields, levels)

    def vmem(*s, dtype=jnp.float32):
        return pltpu.VMEM(s, dtype)

    def flat3(x):
        return x.reshape(-1, rows, cols)

    whole = jax.ShapeDtypeStruct((count, rows, cols), jnp.float32)
    field = vmem(count, rows, cols)
    level = vmem(levels, rows, cols)
    index = vmem(levels, rows, cols, dtype=jnp.int32)
    halo = vmem(pairs, quads, QUAD * HALO, cols)
    g_halo = vmem(4 * levels // QUAD, QUAD * HALO, cols)
    weights = vmem(levels, len(SHIFTS), 32, cols)
    copies = pairs * 12 + 2
    tl, grad = pl.pallas_call(
        functools.partial(kernel, dims, sizes),
        out_shape=(whole, whole),
        in_specs=[ANY] * 8,
        out_specs=(ANY, ANY),
        scratch_shapes=[
            field, field, field, index, index, level, level,
            vmem(fields * (levels - 1), rows, cols), field, field,
            halo, halo, halo, halo,
            vmem(pairs, groups, rows, cols), vmem(pairs, 2, groups, 32, cols),
            g_halo, g_halo, g_halo, g_halo, halo, halo, halo, halo,
            vmem(pairs, groups, rows, cols), vmem(pairs, 2, groups, rows, cols),
            vmem(PAIR * levels, rows, cols), vmem(PAIR * levels, 32, cols),
            vmem(len(SHIFTS), 32, cols), weights, weights, field, field, field, field,
            pltpu.SemaphoreType.DMA((8,)),
            pltpu.SemaphoreType.DMA((2 * pairs,)),
            pltpu.SemaphoreType.DMA((copies,)),
            pltpu.SemaphoreType.DMA((copies,)),
        ],
        compiler_params=pltpu.CompilerParams(
            collective_id=0, has_side_effects=True, vmem_limit_bytes=LIMIT
        ),
    )(
        flat3(increment), flat3(obs_dep), flat3(obs_weight), dep_lon, dep_lat, frac_lon, frac_lat,
        flat3(coupling),
    )
    return tl.reshape(increment.shape), grad.reshape(increment.shape)


def solution(mesh):
    sizes = (mesh.shape["lat"], mesh.shape["lon"])
    wide = P(None, None, "lon", "lat")
    level = P(None, "lon", "lat")
    return jax.shard_map(
        functools.partial(shards, sizes),
        mesh=mesh,
        in_specs=(wide, wide, wide, level, level, level, level, wide),
        out_specs=(wide, wide),
        check_vma=False,
    )
```

```python
import functools

import jax
import jax.numpy as jnp
from jax import lax
from jax.experimental import pallas as pl
from jax.experimental.pallas import tpu as pltpu
from jax.sharding import PartitionSpec as P

HALO = 6
SHIFTS = tuple(range(1 - HALO, HALO + 1))
LANES = 128
SLOT = 16
PER = LANES // SLOT
QUAD = 4
PAIR = 2
MESH = pl.DeviceIdType.MESH
ANY = pl.BlockSpec(memory_space=pl.ANY)
LIMIT = 56 * 1024 * 1024


def lane_index(shape):
    return lax.broadcasted_iota(jnp.int32, shape, len(shape) - 1)


def roll(x, shift):
    return pltpu.roll(x, shift, x.ndim - 1)


def neighbours(sizes):
    lat, lon = lax.axis_index("lat"), lax.axis_index("lon")

    def at(dy, dx):
        return {
            "lat": lax.rem(lat + dy + sizes[0], sizes[0]),
            "lon": lax.rem(lon + dx + sizes[1], sizes[1]),
        }

    return at


def greet(devices):
    barrier = pltpu.get_barrier_semaphore()
    for device in devices:
        pl.semaphore_signal(barrier, inc=1, device_id=device, device_id_type=MESH)
    pl.semaphore_wait(barrier, len(devices))


def remote(src, dst, send, recv, number, device):
    return pltpu.make_async_remote_copy(
        src_ref=src,
        dst_ref=dst,
        send_sem=send.at[number],
        recv_sem=recv.at[number],
        device_id=device,
        device_id_type=MESH,
    )


def pack_edges(src, base, dst):
    @pl.loop(0, dst.shape[0])
    def _(group):
        total = None
        for e in range(PER):
            x = src[base + group * PER + e]
            lane = lane_index(x.shape)
            x = jnp.where((lane < HALO) | (lane >= LANES - HALO), x, 0.0)
            x = roll(x, (HALO + SLOT * e) % LANES)
            total = x if total is None else total + x
        dst[group] = total


def pack_rows(src, base, low, high):
    @pl.loop(0, low.shape[0])
    def _(block):
        for i in range(QUAD):
            at = base + block * QUAD + i
            to = pl.ds(HALO * i, HALO)
            low[block, to] = src[at, 0:HALO].astype(jnp.float32)
            high[block, to] = src[at, 16 - HALO : 16].astype(jnp.float32)


def unpack_rows(src, base, left, right, dst):
    @pl.loop(0, left.shape[0])
    def _(block):
        for i in range(QUAD):
            at = block * QUAD + i
            of = pl.ds(HALO * i, HALO)
            dst[at, 8 - HALO : 8] = left[block, of]
            dst[at, 8:24] = src[base + at]
            dst[at, 24 : 24 + HALO] = right[block, of]


def store_weights(dst, rows, offset, frac):
    rest = 1.0 - frac
    before = None
    for pos, total in enumerate(SHIFTS):
        here = offset == total
        second = 0.0 if before is None else jnp.where(before, frac, 0.0)
        dst[pos, rows] = jnp.where(here, rest, second)
        before = here


def factor(dims, coup, ratio, inverse):
    fields, levels = dims
    previous = [None] * fields
    for k in range(levels):
        for f in range(fields):
            at, c = f * levels + k, f * (levels - 1) + k
            denom = 1.0
            if k > 0:
                below = coup[c - 1]
                denom = denom + below
            if k < levels - 1:
                above = coup[c]
                denom = denom + above
            if k > 0:
                denom = denom - below * previous[f]
            inv = 1.0 / denom
            inverse[at] = inv
            if k < levels - 1:
                previous[f] = above * inv
                ratio[at] = previous[f]


def advect(dims, first_field, band, bands, wide, edges, lonw, latw, coup, inverse, shifted, prime):
    fields, levels = dims
    has_lower = band > 0
    has_upper = band < bands - 1

    @pl.loop(0, levels)
    def _(k):
        lane = lane_index(wide.shape[1:])
        for member in range(PAIR):
            local = member * levels + k
            main = wide[local]
            group, slot = local // PER, local % PER
            shift = lax.rem(2 * LANES - HALO - SLOT * slot, LANES)
            lower = jnp.where(has_lower, roll(edges[0, group], shift), 0.0)
            upper = jnp.where(has_upper, roll(edges[1, group], shift), 0.0)
            edge = jnp.where(lane < LANES // 2, upper, lower)
            for pos, total in enumerate(SHIFTS):
                t = -total
                if t == 0:
                    shifted[member, pos] = main
                    continue
                inside = (lane >= LANES + t) if t < 0 else (lane < t)
                shifted[member, pos] = roll(jnp.where(inside, edge, main), (-t) % LANES)
        first = k == 0
        for half in range(2):
            rows = pl.ds(8 * half, 8)
            inner_rows = pl.ds(8 + 8 * half, 8)
            advected = [None] * PAIR
            for lon_pos, lon_total in enumerate(SHIFTS):
                near = pl.ds(8 + 8 * half - lon_total, 8)
                inner = [None] * PAIR
                for pos in range(len(SHIFTS)):
                    w = latw[k, pos, inner_rows]
                    for member in range(PAIR):
                        term = w * shifted[member, pos, near]
                        inner[member] = term if pos == 0 else inner[member] + term
                w = lonw[k, lon_pos, inner_rows]
                for member in range(PAIR):
                    term = w * inner[member]
                    advected[member] = term if lon_pos == 0 else advected[member] + term
            for member in range(PAIR):
                f = first_field + member
                at, c = f * levels + k, f * (levels - 1) + k
                below = jnp.where(first, 0.0, coup[jnp.where(first, c, c - 1), rows])
                before = jnp.where(first, 0.0, prime[jnp.where(first, at, at - 1), rows])
                prime[at, rows] = (advected[member] + below * before) * inverse[at, rows]


def solve(dims, first_field, prime, ratio, inverse, coup, dep, weight, tl, z):
    fields, levels = dims
    members = range(first_field, first_field + PAIR)
    x = {}
    for k in range(levels - 1, -1, -1):
        for f in members:
            at = f * levels + k
            x[f] = prime[at] if k == levels - 1 else prime[at] + ratio[at] * x[f]
            tl[at] = x[f]
    for k in range(levels):
        for f in members:
            at = f * levels + k
            forcing = weight[at] * (tl[at] - dep[at])
            if k > 0:
                forcing = forcing + coup[f * (levels - 1) + k - 1] * x[f]
            x[f] = forcing * inverse[at]
            prime[at] = x[f]
    for k in range(levels - 1, -1, -1):
        for f in members:
            at = f * levels + k
            x[f] = prime[at] if k == levels - 1 else prime[at] + ratio[at] * x[f]
            z[at] = x[f]


def collect(dims, first_field, wide, lonw, latw, inc, grad, spill):
    fields, levels = dims
    lane = lane_index((8, LANES))

    @pl.loop(0, levels)
    def _(k):
        for half in range(2):
            rows = pl.ds(8 * half, 8)
            sums = {}
            for lon_pos, lon_total in enumerate(SHIFTS):
                near = pl.ds(8 + 8 * half + lon_total, 8)
                scale = lonw[k, lon_pos, near]
                scaled = [scale * wide[f * levels + k, near] for f in range(PAIR)]
                for pos in range(len(SHIFTS)):
                    w = latw[k, pos, near]
                    for f in range(PAIR):
                        term = w * scaled[f]
                        sums[f, pos] = term if lon_pos == 0 else sums[f, pos] + term
            for f in range(PAIR):
                at = (first_field + f) * levels + k
                total, outside = inc[at, rows], jnp.zeros((8, LANES), jnp.float32)
                for pos, n in enumerate(SHIFTS):
                    if n == 0:
                        total = total + sums[f, pos]
                        continue
                    moved = roll(sums[f, pos], (-n) % LANES)
                    wraps = (lane >= LANES - n) if n > 0 else (lane < -n)
                    total = total + jnp.where(wraps, 0.0, moved)
                    outside = outside + jnp.where(wraps, moved, 0.0)
                grad[at, rows] = total
                spill[f * levels + k, rows] = outside


def finish(base, band, bands, edges, grad):
    has_lower = band > 0
    has_upper = band < bands - 1

    @pl.loop(0, edges.shape[1])
    def _(group):
        lower = jnp.where(has_lower, edges[0, group], 0.0)
        upper = jnp.where(has_upper, edges[1, group], 0.0)
        lane = lane_index(lower.shape)
        for e in range(PER):
            shift = (-HALO - SLOT * e) % LANES
            low = jnp.where(lane < HALO, roll(lower, shift), 0.0)
            high = jnp.where(lane >= LANES - HALO, roll(upper, shift), 0.0)
            at = base + group * PER + e
            grad[at] = grad[at] + (low + high)


def kernel(
    dims, sizes,
    inc_h, dep_h, weight_h, olon_h, olat_h, flon_h, flat_h, coup_h,
    tl_h, grad_h,
    inc, dep, weight, olon, olat, flon, flat, coup, tl, grad,
    low, high, from_left, from_right, edge_out, edge_in,
    g_low, g_high, g_left, g_right, z_low, z_high, z_left, z_right,
    back_out, back_in, spill, wide, shifted, lonw, latw, prime, ratio, inverse, z,
    load_sem, store_sem, send, recv,
):
    fields, levels = dims
    pairs = fields // PAIR
    per_pair = PAIR * levels
    at = neighbours(sizes)
    band, bands = lax.axis_index("lat"), sizes[0]
    numbers = iter(range(send.shape[0]))

    loads = [
        pltpu.make_async_copy(src, dst, load_sem.at[i])
        for i, (src, dst) in enumerate(
            [(inc_h, inc), (olon_h, olon), (olat_h, olat), (flon_h, flon), (flat_h, flat),
             (coup_h, coup), (dep_h, dep), (weight_h, weight)]
        )
    ]
    for load in loads:
        load.start()

    def launch(src, dst, device):
        copy = remote(src, dst, send, recv, next(numbers), device)
        copy.start()
        return copy

    greet([at(dy, dx) for dy in (-1, 0, 1) for dx in (-1, 0, 1) if (dy, dx) != (0, 0)])
    loads[0].wait()
    inward = []
    for pair in range(pairs):
        copies = []
        packed = edge_out.at[pair]
        pack_edges(inc, pair * per_pair, packed)
        for dy in (-1, 1):
            side = edge_in.at[pair, 0 if dy == 1 else 1]
            copies.append(launch(packed.at[:, 0:8], side.at[:, 24:32], at(dy, -1)))
            copies.append(launch(packed.at[:, 8:16], side.at[:, 0:8], at(dy, 1)))
            copies.append(launch(packed, side.at[:, 8:24], at(dy, 0)))
        pack_rows(inc, pair * per_pair, low.at[pair], high.at[pair])
        copies.append(launch(low.at[pair], from_right.at[pair], at(0, -1)))
        copies.append(launch(high.at[pair], from_left.at[pair], at(0, 1)))
        inward.append(copies)
    for load in loads[1:6]:
        load.wait()
    geometry = (olon, olat, flon, flat)
    blocks = levels // QUAD
    for i, own in enumerate(geometry):
        part = pl.ds(i * blocks, blocks)
        pack_rows(own, 0, g_low.at[part], g_high.at[part])
    around = [
        launch(g_low, g_right, at(0, -1)),
        launch(g_high, g_left, at(0, 1)),
    ]

    @pl.loop(0, levels)
    def _(k):
        store_weights(lonw.at[k], pl.ds(8, 16), olon[k], flon[k])
        store_weights(latw.at[k], pl.ds(8, 16), olat[k], flat[k])

    factor(dims, coup, ratio, inverse)
    for load in loads[6:]:
        load.wait()

    stores, across = [], []
    for pair in range(pairs):
        base = pair * per_pair
        for copy in inward[pair]:
            copy.wait()
        unpack_rows(inc, base, from_left.at[pair], from_right.at[pair], wide)
        advect(dims, pair * PAIR, band, bands, wide, edge_in.at[pair], lonw, latw, coup, inverse, shifted, prime)
        solve(dims, pair * PAIR, prime, ratio, inverse, coup, dep, weight, tl, z)
        pack_rows(z, base, z_low.at[pair], z_high.at[pair])
        across.append([
            launch(z_low.at[pair], z_right.at[pair], at(0, -1)),
            launch(z_high.at[pair], z_left.at[pair], at(0, 1)),
        ])
        part = pl.ds(base, per_pair)
        store = pltpu.make_async_copy(tl.at[part], tl_h.at[part], store_sem.at[pair])
        store.start()
        stores.append(store)

    for copy in around:
        copy.wait()

    @pl.loop(0, blocks)
    def _(block):
        for i in range(QUAD):
            k = block * QUAD + i
            of = pl.ds(HALO * i, HALO)
            for side, rows in ((g_left, pl.ds(8 - HALO, HALO)), (g_right, pl.ds(24, HALO))):
                parts = [side[number * blocks + block, of] for number in range(4)]
                store_weights(lonw.at[k], rows, parts[0], parts[2])
                store_weights(latw.at[k], rows, parts[1], parts[3])

    returned = []
    for pair in range(pairs):
        base = pair * per_pair
        for copy in across[pair]:
            copy.wait()
        unpack_rows(z, base, z_left.at[pair], z_right.at[pair], wide)
        collect(dims, pair * PAIR, wide, lonw, latw, inc, grad, spill)
        pack_edges(spill, 0, back_out.at[pair])
        returned.append([
            launch(back_out.at[pair], back_in.at[pair, 1], at(-1, 0)),
            launch(back_out.at[pair], back_in.at[pair, 0], at(1, 0)),
        ])
    for pair in range(pairs):
        base = pair * per_pair
        for copy in returned[pair]:
            copy.wait()
        finish(base, band, bands, back_in.at[pair], grad)
        part = pl.ds(base, per_pair)
        store = pltpu.make_async_copy(grad.at[part], grad_h.at[part], store_sem.at[pairs + pair])
        store.start()
        stores.append(store)
    for store in stores:
        store.wait()


def shards(sizes, increment, obs_dep, obs_weight, dep_lon, dep_lat, frac_lon, frac_lat, coupling):
    fields, levels, rows, cols = increment.shape
    count = fields * levels
    pairs = fields // PAIR
    groups = PAIR * levels // PER
    quads = PAIR * levels // QUAD
    dims = (fields, levels)

    def vmem(*s, dtype=jnp.float32):
        return pltpu.VMEM(s, dtype)

    def flat3(x):
        return x.reshape(-1, rows, cols)

    whole = jax.ShapeDtypeStruct((count, rows, cols), jnp.float32)
    field = vmem(count, rows, cols)
    level = vmem(levels, rows, cols)
    index = vmem(levels, rows, cols, dtype=jnp.int32)
    halo = vmem(pairs, quads, QUAD * HALO, cols)
    g_halo = vmem(4 * levels // QUAD, QUAD * HALO, cols)
    weights = vmem(levels, len(SHIFTS), 32, cols)
    copies = pairs * 12 + 2
    tl, grad = pl.pallas_call(
        functools.partial(kernel, dims, sizes),
        out_shape=(whole, whole),
        in_specs=[ANY] * 8,
        out_specs=(ANY, ANY),
        scratch_shapes=[
            field, field, field, index, index, level, level,
            vmem(fields * (levels - 1), rows, cols), field, field,
            halo, halo, halo, halo,
            vmem(pairs, groups, rows, cols), vmem(pairs, 2, groups, 32, cols),
            g_halo, g_halo, g_halo, g_halo, halo, halo, halo, halo,
            vmem(pairs, groups, rows, cols), vmem(pairs, 2, groups, rows, cols),
            vmem(PAIR * levels, rows, cols), vmem(PAIR * levels, 32, cols),
            vmem(PAIR, len(SHIFTS), 32, cols), weights, weights, field, field, field, field,
            pltpu.SemaphoreType.DMA((8,)),
            pltpu.SemaphoreType.DMA((2 * pairs,)),
            pltpu.SemaphoreType.DMA((copies,)),
            pltpu.SemaphoreType.DMA((copies,)),
        ],
        compiler_params=pltpu.CompilerParams(
            collective_id=0, has_side_effects=True, vmem_limit_bytes=LIMIT
        ),
    )(
        flat3(increment), flat3(obs_dep), flat3(obs_weight), dep_lon, dep_lat, frac_lon, frac_lat,
        flat3(coupling),
    )
    return tl.reshape(increment.shape), grad.reshape(increment.shape)


def solution(mesh):
    sizes = (mesh.shape["lat"], mesh.shape["lon"])
    wide = P(None, None, "lon", "lat")
    level = P(None, "lon", "lat")
    return jax.shard_map(
        functools.partial(shards, sizes),
        mesh=mesh,
        in_specs=(wide, wide, wide, level, level, level, level, wide),
        out_specs=(wide, wide),
        check_vma=False,
    )
```

```python
import functools

import jax
import jax.numpy as jnp
from jax import lax
from jax.experimental import pallas as pl
from jax.experimental.pallas import tpu as pltpu
from jax.sharding import PartitionSpec as P

HALO = 6
SHIFTS = tuple(range(1 - HALO, HALO + 1))
LANES = 128
SLOT = 16
PER = LANES // SLOT
QUAD = 4
PAIR = 2
MESH = pl.DeviceIdType.MESH
ANY = pl.BlockSpec(memory_space=pl.ANY)
LIMIT = 56 * 1024 * 1024


def lane_index(shape):
    return lax.broadcasted_iota(jnp.int32, shape, len(shape) - 1)


def roll(x, shift):
    return pltpu.roll(x, shift, x.ndim - 1)


def neighbours(sizes):
    lat, lon = lax.axis_index("lat"), lax.axis_index("lon")

    def at(dy, dx):
        return {
            "lat": lax.rem(lat + dy + sizes[0], sizes[0]),
            "lon": lax.rem(lon + dx + sizes[1], sizes[1]),
        }

    return at


def greet(devices):
    barrier = pltpu.get_barrier_semaphore()
    for device in devices:
        pl.semaphore_signal(barrier, inc=1, device_id=device, device_id_type=MESH)
    pl.semaphore_wait(barrier, len(devices))


def remote(src, dst, send, recv, number, device):
    return pltpu.make_async_remote_copy(
        src_ref=src,
        dst_ref=dst,
        send_sem=send.at[number],
        recv_sem=recv.at[number],
        device_id=device,
        device_id_type=MESH,
    )


def pack_edges(src, base, dst):
    @pl.loop(0, dst.shape[0])
    def _(group):
        total = None
        for e in range(PER):
            x = src[base + group * PER + e]
            lane = lane_index(x.shape)
            x = jnp.where((lane < HALO) | (lane >= LANES - HALO), x, 0.0)
            x = roll(x, (HALO + SLOT * e) % LANES)
            total = x if total is None else total + x
        dst[group] = total


def pack_rows(src, base, low, high):
    @pl.loop(0, low.shape[0])
    def _(block):
        for i in range(QUAD):
            at = base + block * QUAD + i
            to = pl.ds(HALO * i, HALO)
            low[block, to] = src[at, 0:HALO].astype(jnp.float32)
            high[block, to] = src[at, 16 - HALO : 16].astype(jnp.float32)


def unpack_rows(src, base, left, right, dst):
    @pl.loop(0, left.shape[0])
    def _(block):
        for i in range(QUAD):
            at = block * QUAD + i
            of = pl.ds(HALO * i, HALO)
            dst[at, 8 - HALO : 8] = left[block, of]
            dst[at, 8:24] = src[base + at]
            dst[at, 24 : 24 + HALO] = right[block, of]


def store_weights(dst, rows, offset, frac):
    rest = 1.0 - frac
    before = None
    for pos, total in enumerate(SHIFTS):
        here = offset == total
        second = 0.0 if before is None else jnp.where(before, frac, 0.0)
        dst[pos, rows] = jnp.where(here, rest, second)
        before = here


def factor(dims, coup, ratio, inverse):
    fields, levels = dims
    previous = [None] * fields
    for k in range(levels):
        for f in range(fields):
            at, c = f * levels + k, f * (levels - 1) + k
            denom = 1.0
            if k > 0:
                below = coup[c - 1]
                denom = denom + below
            if k < levels - 1:
                above = coup[c]
                denom = denom + above
            if k > 0:
                denom = denom - below * previous[f]
            inv = 1.0 / denom
            inverse[at] = inv
            if k < levels - 1:
                previous[f] = above * inv
                ratio[at] = previous[f]


def advect(dims, first_field, band, bands, wide, edges, lonw, latw, coup, inverse, shifted, prime):
    fields, levels = dims
    has_lower = band > 0
    has_upper = band < bands - 1

    @pl.loop(0, levels)
    def _(k):
        lane = lane_index(wide.shape[1:])
        for member in range(PAIR):
            local = member * levels + k
            main = wide[local]
            group, slot = local // PER, local % PER
            shift = lax.rem(2 * LANES - HALO - SLOT * slot, LANES)
            lower = jnp.where(has_lower, roll(edges[0, group], shift), 0.0)
            upper = jnp.where(has_upper, roll(edges[1, group], shift), 0.0)
            edge = jnp.where(lane < LANES // 2, upper, lower)
            for pos, total in enumerate(SHIFTS):
                t = -total
                if t == 0:
                    shifted[member, pos] = main
                    continue
                inside = (lane >= LANES + t) if t < 0 else (lane < t)
                shifted[member, pos] = roll(jnp.where(inside, edge, main), (-t) % LANES)
        first = k == 0
        advected = {}
        for start in range(8 - HALO, 16 + HALO):
            users = [(half, 8 + 8 * half - start) for half in range(2) if 8 + 8 * half - start in SHIFTS]
            inner = {}
            for pos in range(len(SHIFTS)):
                sources = [shifted[member, pos, pl.ds(start, 8)] for member in range(PAIR)]
                for half, _ in users:
                    w = latw[k, pos, pl.ds(8 + 8 * half, 8)]
                    for member in range(PAIR):
                        term = w * sources[member]
                        inner[half, member] = term if pos == 0 else inner[half, member] + term
            for half, lon_total in users:
                w = lonw[k, lon_total + HALO - 1, pl.ds(8 + 8 * half, 8)]
                for member in range(PAIR):
                    term = w * inner[half, member]
                    old = advected.get((half, member))
                    advected[half, member] = term if old is None else old + term
        for half in range(2):
            rows = pl.ds(8 * half, 8)
            for member in range(PAIR):
                f = first_field + member
                at, c = f * levels + k, f * (levels - 1) + k
                below = jnp.where(first, 0.0, coup[jnp.where(first, c, c - 1), rows])
                before = jnp.where(first, 0.0, prime[jnp.where(first, at, at - 1), rows])
                prime[at, rows] = (advected[half, member] + below * before) * inverse[at, rows]


def solve(dims, first_field, prime, ratio, inverse, coup, dep, weight, tl, z):
    fields, levels = dims
    members = range(first_field, first_field + PAIR)
    x = {}
    for k in range(levels - 1, -1, -1):
        for f in members:
            at = f * levels + k
            x[f] = prime[at] if k == levels - 1 else prime[at] + ratio[at] * x[f]
            tl[at] = x[f]
    for k in range(levels):
        for f in members:
            at = f * levels + k
            forcing = weight[at] * (tl[at] - dep[at])
            if k > 0:
                forcing = forcing + coup[f * (levels - 1) + k - 1] * x[f]
            x[f] = forcing * inverse[at]
            prime[at] = x[f]
    for k in range(levels - 1, -1, -1):
        for f in members:
            at = f * levels + k
            x[f] = prime[at] if k == levels - 1 else prime[at] + ratio[at] * x[f]
            z[at] = x[f]


def collect(dims, first_field, wide, lonw, latw, inc, grad, spill):
    fields, levels = dims
    lane = lane_index((8, LANES))

    @pl.loop(0, levels)
    def _(k):
        for half in range(2):
            rows = pl.ds(8 * half, 8)
            sums = {}
            for lon_pos, lon_total in enumerate(SHIFTS):
                near = pl.ds(8 + 8 * half + lon_total, 8)
                scale = lonw[k, lon_pos, near]
                scaled = [scale * wide[f * levels + k, near] for f in range(PAIR)]
                for pos in range(len(SHIFTS)):
                    w = latw[k, pos, near]
                    for f in range(PAIR):
                        term = w * scaled[f]
                        sums[f, pos] = term if lon_pos == 0 else sums[f, pos] + term
            for f in range(PAIR):
                at = (first_field + f) * levels + k
                total, outside = inc[at, rows], jnp.zeros((8, LANES), jnp.float32)
                for pos, n in enumerate(SHIFTS):
                    if n == 0:
                        total = total + sums[f, pos]
                        continue
                    moved = roll(sums[f, pos], (-n) % LANES)
                    wraps = (lane >= LANES - n) if n > 0 else (lane < -n)
                    total = total + jnp.where(wraps, 0.0, moved)
                    outside = outside + jnp.where(wraps, moved, 0.0)
                grad[at, rows] = total
                spill[f * levels + k, rows] = outside


def finish(base, band, bands, edges, grad):
    has_lower = band > 0
    has_upper = band < bands - 1

    @pl.loop(0, edges.shape[1])
    def _(group):
        lower = jnp.where(has_lower, edges[0, group], 0.0)
        upper = jnp.where(has_upper, edges[1, group], 0.0)
        lane = lane_index(lower.shape)
        for e in range(PER):
            shift = (-HALO - SLOT * e) % LANES
            low = jnp.where(lane < HALO, roll(lower, shift), 0.0)
            high = jnp.where(lane >= LANES - HALO, roll(upper, shift), 0.0)
            at = base + group * PER + e
            grad[at] = grad[at] + (low + high)


def kernel(
    dims, sizes,
    inc_h, dep_h, weight_h, olon_h, olat_h, flon_h, flat_h, coup_h,
    tl_h, grad_h,
    inc, dep, weight, olon, olat, flon, flat, coup, tl, grad,
    low, high, from_left, from_right, edge_out, edge_in,
    g_low, g_high, g_left, g_right, z_low, z_high, z_left, z_right,
    back_out, back_in, spill, wide, shifted, lonw, latw, prime, ratio, inverse, z,
    load_sem, store_sem, send, recv,
):
    fields, levels = dims
    pairs = fields // PAIR
    per_pair = PAIR * levels
    at = neighbours(sizes)
    band, bands = lax.axis_index("lat"), sizes[0]
    numbers = iter(range(send.shape[0]))

    loads = [
        pltpu.make_async_copy(src, dst, load_sem.at[i])
        for i, (src, dst) in enumerate(
            [(inc_h, inc), (olon_h, olon), (olat_h, olat), (flon_h, flon), (flat_h, flat),
             (coup_h, coup), (dep_h, dep), (weight_h, weight)]
        )
    ]
    for load in loads:
        load.start()

    def launch(src, dst, device):
        copy = remote(src, dst, send, recv, next(numbers), device)
        copy.start()
        return copy

    greet([at(dy, dx) for dy in (-1, 0, 1) for dx in (-1, 0, 1) if (dy, dx) != (0, 0)])
    loads[0].wait()
    inward = []
    for pair in range(pairs):
        copies = []
        packed = edge_out.at[pair]
        pack_edges(inc, pair * per_pair, packed)
        for dy in (-1, 1):
            side = edge_in.at[pair, 0 if dy == 1 else 1]
            copies.append(launch(packed.at[:, 0:8], side.at[:, 24:32], at(dy, -1)))
            copies.append(launch(packed.at[:, 8:16], side.at[:, 0:8], at(dy, 1)))
            copies.append(launch(packed, side.at[:, 8:24], at(dy, 0)))
        pack_rows(inc, pair * per_pair, low.at[pair], high.at[pair])
        copies.append(launch(low.at[pair], from_right.at[pair], at(0, -1)))
        copies.append(launch(high.at[pair], from_left.at[pair], at(0, 1)))
        inward.append(copies)
    for load in loads[1:6]:
        load.wait()
    geometry = (olon, olat, flon, flat)
    blocks = levels // QUAD
    for i, own in enumerate(geometry):
        part = pl.ds(i * blocks, blocks)
        pack_rows(own, 0, g_low.at[part], g_high.at[part])
    around = [
        launch(g_low, g_right, at(0, -1)),
        launch(g_high, g_left, at(0, 1)),
    ]

    @pl.loop(0, levels)
    def _(k):
        store_weights(lonw.at[k], pl.ds(8, 16), olon[k], flon[k])
        store_weights(latw.at[k], pl.ds(8, 16), olat[k], flat[k])

    factor(dims, coup, ratio, inverse)
    for load in loads[6:]:
        load.wait()

    stores, across = [], []
    for pair in range(pairs):
        base = pair * per_pair
        for copy in inward[pair]:
            copy.wait()
        unpack_rows(inc, base, from_left.at[pair], from_right.at[pair], wide)
        advect(dims, pair * PAIR, band, bands, wide, edge_in.at[pair], lonw, latw, coup, inverse, shifted, prime)
        solve(dims, pair * PAIR, prime, ratio, inverse, coup, dep, weight, tl, z)
        pack_rows(z, base, z_low.at[pair], z_high.at[pair])
        across.append([
            launch(z_low.at[pair], z_right.at[pair], at(0, -1)),
            launch(z_high.at[pair], z_left.at[pair], at(0, 1)),
        ])
        part = pl.ds(base, per_pair)
        store = pltpu.make_async_copy(tl.at[part], tl_h.at[part], store_sem.at[pair])
        store.start()
        stores.append(store)

    for copy in around:
        copy.wait()

    @pl.loop(0, blocks)
    def _(block):
        for i in range(QUAD):
            k = block * QUAD + i
            of = pl.ds(HALO * i, HALO)
            for side, rows in ((g_left, pl.ds(8 - HALO, HALO)), (g_right, pl.ds(24, HALO))):
                parts = [side[number * blocks + block, of] for number in range(4)]
                store_weights(lonw.at[k], rows, parts[0], parts[2])
                store_weights(latw.at[k], rows, parts[1], parts[3])

    returned = []
    for pair in range(pairs):
        base = pair * per_pair
        for copy in across[pair]:
            copy.wait()
        unpack_rows(z, base, z_left.at[pair], z_right.at[pair], wide)
        collect(dims, pair * PAIR, wide, lonw, latw, inc, grad, spill)
        pack_edges(spill, 0, back_out.at[pair])
        returned.append([
            launch(back_out.at[pair], back_in.at[pair, 1], at(-1, 0)),
            launch(back_out.at[pair], back_in.at[pair, 0], at(1, 0)),
        ])
    for pair in range(pairs):
        base = pair * per_pair
        for copy in returned[pair]:
            copy.wait()
        finish(base, band, bands, back_in.at[pair], grad)
        part = pl.ds(base, per_pair)
        store = pltpu.make_async_copy(grad.at[part], grad_h.at[part], store_sem.at[pairs + pair])
        store.start()
        stores.append(store)
    for store in stores:
        store.wait()


def shards(sizes, increment, obs_dep, obs_weight, dep_lon, dep_lat, frac_lon, frac_lat, coupling):
    fields, levels, rows, cols = increment.shape
    count = fields * levels
    pairs = fields // PAIR
    groups = PAIR * levels // PER
    quads = PAIR * levels // QUAD
    dims = (fields, levels)

    def vmem(*s, dtype=jnp.float32):
        return pltpu.VMEM(s, dtype)

    def flat3(x):
        return x.reshape(-1, rows, cols)

    whole = jax.ShapeDtypeStruct((count, rows, cols), jnp.float32)
    field = vmem(count, rows, cols)
    level = vmem(levels, rows, cols)
    index = vmem(levels, rows, cols, dtype=jnp.int32)
    halo = vmem(pairs, quads, QUAD * HALO, cols)
    g_halo = vmem(4 * levels // QUAD, QUAD * HALO, cols)
    weights = vmem(levels, len(SHIFTS), 32, cols)
    copies = pairs * 12 + 2
    tl, grad = pl.pallas_call(
        functools.partial(kernel, dims, sizes),
        out_shape=(whole, whole),
        in_specs=[ANY] * 8,
        out_specs=(ANY, ANY),
        scratch_shapes=[
            field, field, field, index, index, level, level,
            vmem(fields * (levels - 1), rows, cols), field, field,
            halo, halo, halo, halo,
            vmem(pairs, groups, rows, cols), vmem(pairs, 2, groups, 32, cols),
            g_halo, g_halo, g_halo, g_halo, halo, halo, halo, halo,
            vmem(pairs, groups, rows, cols), vmem(pairs, 2, groups, rows, cols),
            vmem(PAIR * levels, rows, cols), vmem(PAIR * levels, 32, cols),
            vmem(PAIR, len(SHIFTS), 32, cols), weights, weights, field, field, field, field,
            pltpu.SemaphoreType.DMA((8,)),
            pltpu.SemaphoreType.DMA((2 * pairs,)),
            pltpu.SemaphoreType.DMA((copies,)),
            pltpu.SemaphoreType.DMA((copies,)),
        ],
        compiler_params=pltpu.CompilerParams(
            collective_id=0, has_side_effects=True, vmem_limit_bytes=LIMIT
        ),
    )(
        flat3(increment), flat3(obs_dep), flat3(obs_weight), dep_lon, dep_lat, frac_lon, frac_lat,
        flat3(coupling),
    )
    return tl.reshape(increment.shape), grad.reshape(increment.shape)


def solution(mesh):
    sizes = (mesh.shape["lat"], mesh.shape["lon"])
    wide = P(None, None, "lon", "lat")
    level = P(None, "lon", "lat")
    return jax.shard_map(
        functools.partial(shards, sizes),
        mesh=mesh,
        in_specs=(wide, wide, wide, level, level, level, level, wide),
        out_specs=(wide, wide),
        check_vma=False,
    )
```
